512 devices in a mesh: dp: 8 (over x, y_hi), expert: 64 (over y_lo, z, core).
Axes of the slice: x: 4, y: 8 (y_hi: 2, y_lo: 4; y = y_hi * 4 + y_lo), z: 8, core: 2. Of those that a mesh axis runs over, the one named last changes fastest.
Arguments:
- tokens: bfloat16 [65536, 3584], P(('dp', 'expert')), may hold values from -6 to 6
- out_grad: bfloat16 [65536, 3584], P(('dp', 'expert')), may hold values from -1.1953125 to 1.1953125
- gate_weight: bfloat16 [3584, 32768], P('dp', 'expert'), may hold values from -0.09375 to 0.09375
- up_weight: bfloat16 [3584, 32768], P('dp', 'expert'), may hold values from -0.09375 to 0.09375
- route_ids: int32 [65536, 8], P(('dp', 'expert')), may hold values from 0 to 255, all different within a row; in each aligned block of 128 rows (0 to 127, 128 to 255, ...) at most 6 rows name the same one
- route_weights: float32 [65536, 8], P(('dp', 'expert')), may hold values from 0.02 to 0.5
Outputs:
- grad_down: bfloat16 [32768, 3584], P(('expert', 'dp'))
The draws below stay inside these ranges and needn't reach their ends.
Inputs may be any that keep to these rules, and one draw needn't show every extreme that they name: `route_ids`: each row names 8 different experts. At most 6 of the rows of one device name any one expert, a bound that some block reaches.
All inputs are finite; a program needn't handle non-finite values.
Results may differ from the reference program's by a relative error of at most 0.015.
Values may be sent and summed in bfloat16 or wider, within the bound.
A program may use at most 128 MiB of HBM per device.

```python
import math
from functools import partial
import jax
import jax.numpy as jnp
import numpy as np
from jax import lax

DW = 3584
FF = 2048
N_ROUTED = 256
TOPK = 8
TOK_DEV = 128
CAP = 6
EXPERTS = 16
TOKENS = 65536
N_DP = 8
N_EXPERT = 64


def shard_levels(own_key, extent, split, smallest, largest):
    gain = 1.0
    for axis_at, blocks in split:
        draws = jax.random.uniform(jax.random.fold_in(jax.random.fold_in(own_key, 6), axis_at), (blocks,), jnp.float32, smallest / len(split), largest / len(split))
        gain = gain * jnp.repeat(jnp.exp(draws), extent[axis_at] // blocks).reshape((-1,) + (1,) * (len(extent) - 1 - axis_at))
    return gain


def routed_block(rng, own, number, rows, count, top, limit, slope):
    ranking = jax.random.permutation(rng, count)
    packed, usual = load_shares(count, rows * top, limit, slope, True), load_shares(count, rows * top, limit, slope, False)
    places = jnp.arange(count)

    def named(lengths, offset_by):
        used = int((lengths > 0).sum())
        fixed = max(1, used // 4)
        moved = fixed + (places - fixed + offset_by * (used - fixed)) % max(1, count - fixed)
        return jnp.zeros((count,), jnp.int32).at[ranking[jnp.where(places < fixed, places, moved)]].set(jnp.asarray(lengths, jnp.int32))

    lengths = jnp.where(number % 4 == 0, named(packed, number // 4), named(usual, number - number // 4 - 1))
    mixed = jax.random.permutation(jax.random.fold_in(own, 3), count)
    source_of, receiver = mixed[0:count // 2 * 2:2], mixed[1:count // 2 * 2:2]
    margin = jnp.minimum(lengths[source_of] - 1, limit - lengths[receiver]) // 2
    margin = jnp.where((source_of == ranking[0]) | (receiver == ranking[0]) | (lengths[receiver] == 0), 0, jnp.maximum(margin, 0))
    moved = jax.random.randint(jax.random.fold_in(own, 4), (count // 2,), 0, 1 << 20) % (margin + 1)
    lengths = lengths.at[source_of].add(-moved).at[receiver].add(moved)
    labels = jnp.searchsorted(jnp.cumsum(lengths), jnp.arange(rows * top), side="right").astype(jnp.int32)
    listing = labels.reshape(top, rows).T
    listing = listing[jax.random.permutation(jax.random.fold_in(own, 1), rows)]
    offset_by = jax.random.randint(jax.random.fold_in(own, 2), (rows, 1), 0, top)
    return jnp.take_along_axis(listing, (jnp.arange(top)[None, :] + offset_by) % top, axis=1)


def load_shares(count, total, bound, lean, full):
    weights = [(1 << 20) // math.isqrt(standing ** lean) + 1 for standing in range(1, count + 1)]
    largest = bound if full else min(bound, max(-(-total // count), total * weights[0] // sum(weights)))
    least = 1 if total - largest >= count - 1 else 0
    holding, rest = [largest] + [least] * (count - 1), total - largest - least * (count - 1)
    while rest > 0:
        movable = [i for i in range(1, count) if holding[i] < largest] or [i for i in range(1, count) if holding[i] < bound]
        whole, remaining = sum([weights[i] for i in movable]), rest
        for i in movable:
            extra = min(bound - holding[i], max(1, remaining * weights[i] // whole), rest)
            holding[i] = holding[i] + extra
            rest = rest - extra
    return np.array(holding)


def gaussian(own_key, extent, width, bound, split=(), held_as=jnp.bfloat16):
    drawn = width * jax.random.normal(own_key, extent, jnp.float32)
    if split:
        drawn = drawn * shard_levels(own_key, extent, split, -0.22, 0.18)
    return jnp.clip(drawn, -bound, bound).astype(held_as)


def setup_inputs(seed: int = 0) -> dict:
    arg_keys = jax.random.split(jax.random.key(seed), 7)
    tokens = gaussian(arg_keys[0], (TOKENS, DW), 1.0, 6.0, ((0, 512),))
    out_grad = gaussian(arg_keys[1], (TOKENS, DW), 0.2, 1.1953125, ((0, 512),))
    gate_weight = gaussian(arg_keys[2], (DW, EXPERTS * FF), DW ** -0.5, 0.09375, ((0, 8), (1, 64)))
    up_weight = gaussian(arg_keys[3], (DW, EXPERTS * FF), DW ** -0.5, 0.09375, ((0, 8), (1, 64)))
    route_ids_keys = jax.random.split(jax.random.fold_in(arg_keys[4], 1), TOKENS // TOK_DEV)
    route_ids_turns = jax.random.permutation(jax.random.fold_in(arg_keys[4], 3), TOKENS // TOK_DEV)
    route_ids = jax.vmap(lambda own, number: routed_block(jax.random.fold_in(arg_keys[4], 2), own, number, TOK_DEV, N_ROUTED, TOPK, CAP, 2))(route_ids_keys, route_ids_turns).reshape((TOKENS, TOPK))
    route_weights = jnp.clip(jnp.exp(math.log(0.5) - 3.218876 * jax.random.uniform(arg_keys[5], (TOKENS, TOPK), jnp.float32) ** shard_levels(arg_keys[5], (TOKENS, TOPK), ((0, 512),), -0.2, 0.2)), 0.02, 0.5)
    return {"tokens": tokens, "out_grad": out_grad, "gate_weight": gate_weight, "up_weight": up_weight, "route_ids": route_ids, "route_weights": route_weights}


def expert_part(expert, group_tokens, group_grads, group_ids, group_weights, gate_weight, up_weight):
    slot_count = N_EXPERT * CAP
    matches = group_ids == expert
    chosen = jnp.any(matches, axis=1)
    scales = jnp.sum(jnp.where(matches, group_weights, 0.0), axis=1)
    picked = jnp.nonzero(chosen, size=slot_count, fill_value=0)[0]
    filled = jnp.arange(slot_count) < jnp.sum(chosen.astype(jnp.int32))
    routed = jnp.where(filled[:, None], group_tokens[picked], jnp.zeros((), jnp.bfloat16))
    scaled = jnp.where(filled[:, None], scales[picked][:, None] * group_grads[picked].astype(jnp.float32), 0.0)
    scaled = scaled.astype(jnp.bfloat16)
    start_col = (expert * FF).astype(jnp.int32)
    gate_cols = lax.dynamic_slice_in_dim(gate_weight, start_col, FF, 1)
    up_cols = lax.dynamic_slice_in_dim(up_weight, start_col, FF, 1)
    gate_pre = jnp.dot(routed, gate_cols, preferred_element_type=jnp.float32)
    up_pre = jnp.dot(routed, up_cols, preferred_element_type=jnp.float32)
    hidden = (jax.nn.silu(gate_pre) * up_pre).astype(jnp.bfloat16)
    return jnp.dot(hidden.T, scaled, preferred_element_type=jnp.float32).astype(jnp.bfloat16)


def reference(tokens, out_grad, gate_weight, up_weight, route_ids, route_weights):
    group_rows = N_EXPERT * TOK_DEV
    token_groups = tokens.reshape(N_DP, group_rows, DW)
    grad_groups = out_grad.reshape(N_DP, group_rows, DW)
    id_groups = route_ids.reshape(N_DP, group_rows, TOPK)
    weight_groups = route_weights.reshape(N_DP, group_rows, TOPK)

    def group_step(running, group_data):
        group_tokens, group_grads, group_ids, group_weights = group_data
        worker = partial(expert_part, group_tokens=group_tokens, group_grads=group_grads, group_ids=group_ids, group_weights=group_weights, gate_weight=gate_weight, up_weight=up_weight)
        partials = lax.map(worker, jnp.arange(EXPERTS, dtype=jnp.int32))
        return running + partials.astype(jnp.float32), None

    start_sum = jnp.zeros((EXPERTS, FF, DW), jnp.float32)
    summed, _ = lax.scan(group_step, start_sum, (token_groups, grad_groups, id_groups, weight_groups))
    return summed.reshape(EXPERTS * FF, DW).astype(jnp.bfloat16)
```

```python
import jax
import jax.numpy as jnp
from jax import lax
from jax.experimental import pallas as pl
from jax.experimental.pallas import tpu as pltpu
from jax.sharding import PartitionSpec as P

MESH = pl.DeviceIdType.MESH
F32 = jnp.float32
BF16 = jnp.bfloat16

TOK = 128
DW = 3584
SH = 448
COLS = 512
CAP = 6
NK = 4
TILE = 512
SCHEDULE = (
    "O0", "O1", "D0", "D1", "O2", "D2", "O3", "D3", "S0", "S1", "S2", "S3", "Z0", "Z1",
    "D4", "D5", "Z2", "Z3", "D6", "D7", "Z4", "Z5", "Y0", "P0", "Z6", "Z7", "Y1", "X", "C0",
    "P1", "Y2", "A0", "C1", "P2", "B0", "A1", "Y3", "C2", "P3", "B1", "A2", "C3", "B2",
    "A3", "B3", "E0", "E1", "E2", "E3",
)


def kernel(
    ids_ref, rw_ref, tok_hbm, og_hbm, gw_hbm, uw_hbm, out_ref,
    tok, raw, give, take, send_rows, rows, flat, wts, acc, hid_t, part, hop1, hop2, y_out, y_in, fin,
    local_sem, t_recv, y_recv, o_recv, p_recv, fo_recv, fp_recv,
    d_recv, z_recv, c_recv, h1_recv, h2_recv, ry_recv, send_sem,
):
    dp = lax.axis_index("dp")
    ex = lax.axis_index("expert")
    x, yh = dp // 2, lax.rem(dp, 2)
    yl, z, c = ex // 16, lax.rem(ex // 2, 8), lax.rem(ex, 2)
    zp, par = z // 2, lax.rem(z, 2)

    def dev(x_, yh_, yl_, z_, c_):
        return (x_ * 2 + yh_, (yl_ * 8 + z_) * 2 + c_)

    def ring(x_, d):
        return lax.rem(x_ + d + 4, 4)

    sides = (dev(ring(x, 1), yh, yl, z, c), dev(ring(x, -1), yh, yl, z, c))
    y_dev = dev(x, 1 - yh, yl, z, c)
    z_dev = dev(x, yh, yl, z + 1 - 2 * par, c)
    c_dev = dev(x, yh, yl, z, 1 - c)

    def copy(src, dst, sends, recv, to):
        return pltpu.make_async_remote_copy(
            src_ref=src, dst_ref=dst, send_sem=send_sem.at[sends], recv_sem=recv,
            device_id=to, device_id_type=MESH,
        )

    local = [
        pltpu.make_async_copy(tok_hbm, tok.at[0], local_sem.at[0]),
        pltpu.make_async_copy(og_hbm, tok.at[1], local_sem.at[1]),
        pltpu.make_async_copy(gw_hbm, raw.at[0], local_sem.at[2]),
        pltpu.make_async_copy(uw_hbm, raw.at[1], local_sem.at[3]),
    ]
    for one in local:
        one.start()

    barrier = pltpu.get_barrier_semaphore()

    def greet(to):
        pl.semaphore_signal(barrier, inc=1, device_id=to, device_id_type=MESH)

    for to in (*sides, y_dev, z_dev, c_dev):
        greet(to)
    pair = lax.rem(zp + 3 + 2 * par, 4)
    from_z = (z, 2 * pair, 2 * pair + 1, 2 * lax.rem(zp + 2, 4) + 1 - par)
    odd_out = lax.rem(c + yl + zp, 2)
    odd_in = odd_out
    for jj in range(2):
        for zi in range(4):
            to = dev(x, yh, lax.rem(yl + 8 - odd_in - 2 * jj, 4), from_z[zi], c)
            if jj or zi:
                greet(to)
            else:
                pl.when(odd_in == 1)(lambda to=to: greet(to))
    pl.semaphore_wait(barrier, 12 + odd_out)

    row = lax.broadcasted_iota(jnp.int32, (96, TOK), 0)
    row12 = jnp.zeros((96, TOK), jnp.int32)
    for i in range(1, 8):
        row12 = row12 + jnp.where(row >= 12 * i, 1, 0)
    slot = row - 12 * row12
    is_grad = slot >= CAP
    slot = jnp.where(is_grad, slot - CAP, slot)
    earlier = jnp.where(
        lax.broadcasted_iota(jnp.int32, (TOK, TOK), 0)
        < lax.broadcasted_iota(jnp.int32, (TOK, TOK), 1),
        1.0,
        0.0,
    ).astype(BF16)

    def choice(odd):
        to_zp = (zp + odd + 2 * (row12 >> 2)) & 3
        expert = ((yl + (row12 & 3)) & 3) * 4 + to_zp
        named = jnp.zeros((96, TOK), F32)
        scale = jnp.zeros((96, TOK), F32)
        for k in range(8):
            hit = ids_ref[k : k + 1, :] == expert
            named = jnp.where(hit, 1.0, named)
            scale = scale + jnp.where(hit, rw_ref[k : k + 1, :], 0.0)
        rank = jnp.dot(named.astype(BF16), earlier, preferred_element_type=F32)
        pick = jnp.where(rank == slot.astype(F32), named, 0.0)
        slot_scale = jnp.sum(pick * scale, axis=1, keepdims=True)
        saved = jnp.where(is_grad, 0.0, pick).astype(BF16)
        grads = jnp.where(is_grad, pick, 0.0).astype(BF16)

        def rows_of(at):
            got = jnp.dot(saved, tok[0, :, at], preferred_element_type=F32)
            scaled = jnp.dot(grads, tok[1, :, at], preferred_element_type=F32) * slot_scale
            return (got + scaled).astype(BF16)

        return rows_of

    theirs_of, mine_of = choice(1 - odd_out), choice(odd_out)
    local[0].wait()
    local[1].wait()

    @pl.loop(0, DW // TILE)
    def _(n):
        at = pl.ds(pl.multiple_of(n * TILE, TILE), TILE)
        give[0, :, at] = theirs_of(at)

    copy(give.at[0], take, 13, t_recv.at[0], c_dev).start()

    @pl.loop(0, DW // TILE)
    def _(n):
        at = pl.ds(pl.multiple_of(n * TILE, TILE), TILE)
        give[1, :, at] = mine_of(at)

    local[2].wait()
    local[3].wait()

    def block(owner_x, owner_yh, half=None):
        at = (owner_x * 2 + owner_yh) * SH + (0 if half is None else half * (SH // 2))
        size = SH if half is None else SH // 2
        return pl.ds(pl.multiple_of(at, SH // 2), size)

    mine, theirs = block(x, yh), block(x, 1 - yh)
    lane = lax.broadcasted_iota(jnp.int32, (COLS, 128), 1)
    column = lax.broadcasted_iota(jnp.int32, (COLS, 128), 0) - (lane >> 4) * 64 - (lane & 15)
    for k in range(NK):
        order = jnp.where(column == k * 16, 1.0, 0.0).astype(BF16)
        for a in range(2):
            wts[k, mine, a * 128 : (a + 1) * 128] = jnp.dot(
                raw[a], order, preferred_element_type=F32
            ).astype(BF16)
        for s in range(2):
            copy(wts.at[k, mine], wts.at[k, mine], 3, o_recv.at[s, k], sides[s]).start()

    place = lax.broadcasted_iota(jnp.int32, (192, 96), 0)
    source = lax.broadcasted_iota(jnp.int32, (192, 96), 1)
    place24 = jnp.zeros((192, 96), jnp.int32)
    for i in range(1, 8):
        place24 = place24 + jnp.where(place >= 24 * i, 1, 0)
    within = place - 24 * place24
    grad12 = jnp.where(within >= 12, 1, 0)
    within = within - 12 * grad12
    second = jnp.where(within >= CAP, 1, 0)
    wanted = place24 * 12 + grad12 * CAP + within - CAP * second
    own_place = jnp.where((wanted == source) & (second == 0), 1.0, 0.0).astype(BF16)
    other_place = jnp.where((wanted == source) & (second == 1), 1.0, 0.0).astype(BF16)
    copy(give.at[0], take, 13, t_recv.at[0], c_dev).wait_recv()

    @pl.loop(0, DW // TILE)
    def _(n):
        at = pl.ds(pl.multiple_of(n * TILE, TILE), TILE)
        both = jnp.dot(own_place, give[1, :, at], preferred_element_type=F32) + jnp.dot(
            other_place, take[:, at], preferred_element_type=F32
        )
        send_rows[:, :, :, at] = both.astype(BF16).reshape(8, 3, 8, TILE)

    quarter = c * 16 + par * 8
    for dyl in range(4):
        for j in range(2):
            to_yl, to_zp = lax.rem(yl + dyl, 4), lax.rem(zp + odd_out + 2 * j, 4)
            if j == 0:
                zi, to_par = odd_out * (1 + par), (1 - odd_out) * par
            else:
                zi = 3 + odd_out * (par - 2)
                to_par = (1 - odd_out) * (1 - par) + odd_out
            src = send_rows.at[j * 4 + dyl]
            number = (dyl // 2) * 4 + zi
            dst = rows.at[c * 16 + to_par * 8 + number]
            to = dev(x, yh, to_yl, 2 * to_zp + to_par, c)
            remote = copy(src, dst, 0, d_recv.at[number], to)
            if dyl or j:
                remote.start()
            else:
                pl.when(odd_out == 1)(remote.start)

                @pl.when(odd_out == 0)
                def _():
                    pltpu.make_async_copy(src, dst, d_recv.at[0]).start()

    def pass_on(k, of_yh, recv, recv_next, sends):
        for s in range(2):
            of_x = ring(x, (-1, 1)[s])
            whole, half = block(of_x, of_yh), block(of_x, of_yh, s)
            copy(wts.at[k, whole], wts.at[k, whole], 3, recv.at[s, k], sides[s]).wait_recv()
            copy(wts.at[k, half], wts.at[k, half], sends, recv_next.at[s, k], sides[s]).start()

    def event_o(k):
        pass_on(k, yh, o_recv, fo_recv, 5)

    def event_p(k):
        pass_on(k, 1 - yh, p_recv, fp_recv, 5)

    def event_s(k):
        copy(wts.at[k, mine], wts.at[k, mine], 2, y_recv.at[k], y_dev).start()

    def event_y(k):
        copy(wts.at[k, theirs], wts.at[k, theirs], 2, y_recv.at[k], y_dev).wait_recv()
        for s in range(2):
            copy(wts.at[k, theirs], wts.at[k, theirs], 4, p_recv.at[s, k], sides[s]).start()

    def flatten(first, count):
        at = pl.ds(pl.multiple_of(first * 16, 16), count * 16)
        for a in range(2):
            flat[a, at, :] = rows[pl.ds(first, count), a : a + 2].reshape(count * 16, DW)

    def event_d(number):
        at = quarter + number
        copy(rows.at[at], rows.at[at], 0, d_recv.at[number], z_dev).wait_recv()
        copy(rows.at[at], rows.at[at], 6, z_recv.at[number], z_dev).start()
        copy(rows.at[at], rows.at[at], 8, c_recv.at[0], c_dev).start()
        flatten(at, 1)

    def event_z(number):
        at = c * 16 + (1 - par) * 8 + number
        copy(rows.at[at], rows.at[at], 6, z_recv.at[number], z_dev).wait_recv()
        copy(rows.at[at], rows.at[at], 8, c_recv.at[0], c_dev).start()
        flatten(at, 1)

    def event_x():
        at = pl.ds((1 - c) * 16, 16)
        copy(rows.at[at], rows.at[at], 8, c_recv.at[0], c_dev).wait_recv()

        @pl.loop(0, 8)
        def _(n):
            flatten((1 - c) * 16 + n * 2, 2)

    def owned(of_x, of_yh=None):
        at = of_x * 32 + (0 if of_yh is None else of_yh * 16)
        return pl.ds(pl.multiple_of(at, 16), 32 if of_yh is None else 16)

    def event_c(k):
        for s in range(2):
            for of_yh, recv in ((yh, fo_recv), (1 - yh, fp_recv)):
                half = block(ring(x, 2), of_yh, s)
                copy(wts.at[k, half], wts.at[k, half], 5, recv.at[s, k], sides[s]).wait_recv()
        acc[...] = jnp.zeros_like(acc)

        @pl.loop(0, DW // TILE)
        def _(n):
            at = pl.ds(pl.multiple_of(n * TILE, TILE), TILE)
            acc[...] += jnp.dot(flat[0, :, at], wts[k, at, :], preferred_element_type=F32)

        gate, up = acc[:, 0:128], acc[:, 128:256]
        hidden = jnp.transpose(gate / (1.0 + jnp.exp(-gate)) * up)
        hidden = pltpu.roll(hidden, 4, 1)
        lane16 = lax.broadcasted_iota(jnp.int32, hidden.shape, 1) & 15
        hid_t[...] = jnp.where(lane16 >= 4, hidden, 0.0).astype(BF16)

        @pl.loop(0, DW // TILE)
        def _(n):
            at = pl.ds(pl.multiple_of(n * TILE, TILE), TILE)
            part[k, :, at] = jnp.dot(
                hid_t[...], flat[1, :, at], preferred_element_type=F32
            ).astype(BF16)

        for s in range(2):
            copy(
                part.at[k, owned(ring(x, 2), s)], hop1.at[s, k], 10, h1_recv.at[s, k], sides[s]
            ).start()

    def event_a(k):
        for s in range(2):
            copy(hop1.at[s, k], hop1.at[s, k], 10, h1_recv.at[s, k], sides[s]).wait_recv()
            of_x = ring(x, (1, -1)[s])
            at = owned(of_x, s)
            part[k, at, :] = (
                part[k, at, :].astype(F32) + hop1[s, k].astype(F32)
            ).astype(BF16)
            copy(
                part.at[k, owned(of_x)], hop2.at[s, k], 11, h2_recv.at[s, k], sides[s]
            ).start()

    def event_b(k):
        for s in range(2):
            copy(hop2.at[s, k], hop2.at[s, k], 11, h2_recv.at[s, k], sides[s]).wait_recv()

        def total(of_yh):
            at = pl.ds(pl.multiple_of(of_yh * 16, 16), 16)
            return (
                part[k, owned(x, of_yh), :].astype(F32)
                + hop2[0, k, at, :].astype(F32)
                + hop2[1, k, at, :].astype(F32)
            )

        y_out[k] = total(1 - yh).astype(BF16)
        copy(y_out.at[k], y_in.at[k], 12, ry_recv.at[k], y_dev).start()
        fin[k] = total(yh)

    def event_e(k):
        copy(y_out.at[k], y_in.at[k], 12, ry_recv.at[k], y_dev).wait_recv()
        out_ref[k * 16 : (k + 1) * 16, :] = (fin[k] + y_in[k].astype(F32)).astype(BF16)

    events = dict(
        O=event_o, P=event_p, Y=event_y, S=event_s, D=event_d, Z=event_z, C=event_c,
        A=event_a, B=event_b, E=event_e,
    )
    for name in SCHEDULE:
        if name == "X":
            event_x()
        else:
            events[name[0]](int(name[1]))

    def sent(ref, sends, to):
        copy(ref, ref, sends, o_recv.at[0, 0], to).wait_send()

    sent(give.at[0], 13, c_dev)
    sent(rows.at[pl.ds(0, 8)], 6, z_dev)
    sent(rows.at[pl.ds(0, 16)], 8, c_dev)
    pl.when(odd_out == 0)(lambda: sent(rows.at[pl.ds(0, 7)], 0, z_dev))
    pl.when(odd_out == 1)(lambda: sent(rows.at[pl.ds(0, 8)], 0, z_dev))
    sent(wts.at[0, pl.ds(0, 4 * SH)], 2, y_dev)
    for sends in (3, 4, 5):
        sent(wts.at[0], sends, sides[0])
    sent(flat.at[0, pl.ds(0, 128)], 10, sides[0])
    sent(flat.at[0, pl.ds(0, 256)], 11, sides[0])
    sent(flat.at[0, pl.ds(0, 64)], 12, y_dev)


def per_device(tokens, out_grad, gate_weight, up_weight, route_ids, route_weights):
    vmem = pl.BlockSpec(memory_space=pltpu.VMEM)
    anywhere = pl.BlockSpec(memory_space=pl.ANY)
    dma = pltpu.SemaphoreType.DMA
    return pl.pallas_call(
        kernel,
        out_shape=jax.ShapeDtypeStruct((NK * 16, DW), BF16),
        in_specs=[vmem, vmem, anywhere, anywhere, anywhere, anywhere],
        out_specs=vmem,
        scratch_shapes=[
            pltpu.VMEM((2, TOK, DW), BF16),
            pltpu.VMEM((2, SH, COLS), BF16),
            pltpu.VMEM((2, 96, DW), BF16),
            pltpu.VMEM((96, DW), BF16),
            pltpu.VMEM((8, 3, 8, DW), BF16),
            pltpu.VMEM((32, 3, 8, DW), BF16),
            pltpu.VMEM((2, 512, DW), BF16),
            pltpu.VMEM((NK, 8 * SH, 256), BF16),
            pltpu.VMEM((512, 256), F32),
            pltpu.VMEM((128, 512), BF16),
            pltpu.VMEM((NK, 128, DW), BF16),
            pltpu.VMEM((2, NK, 16, DW), BF16),
            pltpu.VMEM((2, NK, 32, DW), BF16),
            pltpu.VMEM((NK, 16, DW), BF16),
            pltpu.VMEM((NK, 16, DW), BF16),
            pltpu.VMEM((NK, 16, DW), F32),
            dma((4,)),
            dma((1,)),
            dma((NK,)),
            dma((2, NK)),
            dma((2, NK)),
            dma((2, NK)),
            dma((2, NK)),
            dma((8,)),
            dma((8,)),
            dma((1,)),
            dma((2, NK)),
            dma((2, NK)),
            dma((NK,)),
            dma((14,)),
        ],
        compiler_params=pltpu.CompilerParams(
            collective_id=0, has_side_effects=True, vmem_limit_bytes=56 << 20
        ),
        name="routed_grad",
    )(route_ids.T, route_weights.T, tokens, out_grad, gate_weight, up_weight)


def solution(mesh):
    return jax.shard_map(
        per_device,
        mesh=mesh,
        in_specs=(
            P(("dp", "expert"), None),
            P(("dp", "expert"), None),
            P("dp", "expert"),
            P("dp", "expert"),
            P(("dp", "expert"), None),
            P(("dp", "expert"), None),
        ),
        out_specs=P(("expert", "dp"), None),
        check_vma=False,
    )
```

```python
import jax
import jax.numpy as jnp
from jax import lax
from jax.experimental import pallas as pl
from jax.experimental.pallas import tpu as pltpu
from jax.sharding import PartitionSpec as P

MESH = pl.DeviceIdType.MESH
F32 = jnp.float32
BF16 = jnp.bfloat16

TOK = 128
DW = 3584
SH = 448
COLS = 512
CAP = 6
NK = 4
TILE = 512
SCHEDULE = (
    "S0", "U0", "U1", "R", "O0", "U2", "D0", "D1", "O1", "U3", "D2", "Y0", "S1", "P0", "D3",
    "Z0", "Z1", "O2", "D4", "D5", "O3", "Z2", "Z3", "D6", "D7", "Y1", "S2", "P1", "Z4",
    "Z5", "Y2", "S3", "P2", "Z6", "Z7", "Y3", "P3", "X", "C0", "C1", "A0", "C2", "A1", "B0",
    "C3", "A2", "B1", "A3", "B2", "B3", "E0", "E1", "E2", "E3",
)


def kernel(
    ids_ref, rw_ref, tok_hbm, og_hbm, gw_hbm, uw_hbm, out_ref,
    tok, raw, give, take, send_rows, rows, flat, wts, acc, hid_t, part, hop1, hop2, y_out, y_in, fin,
    local_sem, t_recv, y_recv, o_recv, p_recv, fo_recv, fp_recv,
    d_recv, z_recv, c_recv, h1_recv, h2_recv, ry_recv, send_sem,
):
    dp = lax.axis_index("dp")
    ex = lax.axis_index("expert")
    x, yh = dp // 2, lax.rem(dp, 2)
    yl, z, c = ex // 16, lax.rem(ex // 2, 8), lax.rem(ex, 2)
    zp, par = z // 2, lax.rem(z, 2)

    def dev(x_, yh_, yl_, z_, c_):
        return (x_ * 2 + yh_, (yl_ * 8 + z_) * 2 + c_)

    def ring(x_, d):
        return lax.rem(x_ + d + 4, 4)

    sides = (dev(ring(x, 1), yh, yl, z, c), dev(ring(x, -1), yh, yl, z, c))
    y_dev = dev(x, 1 - yh, yl, z, c)
    z_dev = dev(x, yh, yl, z + 1 - 2 * par, c)
    c_dev = dev(x, yh, yl, z, 1 - c)

    def copy(src, dst, sends, recv, to):
        return pltpu.make_async_remote_copy(
            src_ref=src, dst_ref=dst, send_sem=send_sem.at[sends], recv_sem=recv,
            device_id=to, device_id_type=MESH,
        )

    local = [
        pltpu.make_async_copy(tok_hbm, tok.at[0], local_sem.at[0]),
        pltpu.make_async_copy(og_hbm, tok.at[1], local_sem.at[1]),
        pltpu.make_async_copy(gw_hbm, raw.at[0], local_sem.at[2]),
        pltpu.make_async_copy(uw_hbm, raw.at[1], local_sem.at[3]),
    ]
    for one in local:
        one.start()

    barrier = pltpu.get_barrier_semaphore()

    def greet(to):
        pl.semaphore_signal(barrier, inc=1, device_id=to, device_id_type=MESH)

    for to in (*sides, y_dev, z_dev, c_dev):
        greet(to)
    pair = lax.rem(zp + 3 + 2 * par, 4)
    from_z = (z, 2 * pair, 2 * pair + 1, 2 * lax.rem(zp + 2, 4) + 1 - par)
    odd_out = lax.rem(c + yl + zp, 2)
    odd_in = odd_out
    for jj in range(2):
        for zi in range(4):
            to = dev(x, yh, lax.rem(yl + 8 - odd_in - 2 * jj, 4), from_z[zi], c)
            if jj or zi:
                greet(to)
            else:
                pl.when(odd_in == 1)(lambda to=to: greet(to))

    row = lax.broadcasted_iota(jnp.int32, (96, TOK), 0)
    row12 = jnp.zeros((96, TOK), jnp.int32)
    for i in range(1, 8):
        row12 = row12 + jnp.where(row >= 12 * i, 1, 0)
    slot = row - 12 * row12
    is_grad = slot >= CAP
    slot = jnp.where(is_grad, slot - CAP, slot)
    earlier = jnp.where(
        lax.broadcasted_iota(jnp.int32, (TOK, TOK), 0)
        < lax.broadcasted_iota(jnp.int32, (TOK, TOK), 1),
        1.0,
        0.0,
    ).astype(BF16)

    def choice(odd):
        to_zp = (zp + odd + 2 * (row12 >> 2)) & 3
        expert = ((yl + (row12 & 3)) & 3) * 4 + to_zp
        named = jnp.zeros((96, TOK), F32)
        scale = jnp.zeros((96, TOK), F32)
        for k in range(8):
            hit = ids_ref[k : k + 1, :] == expert
            named = jnp.where(hit, 1.0, named)
            scale = scale + jnp.where(hit, rw_ref[k : k + 1, :], 0.0)
        rank = jnp.dot(named.astype(BF16), earlier, preferred_element_type=F32)
        pick = jnp.where(rank == slot.astype(F32), named, 0.0)
        slot_scale = jnp.sum(pick * scale, axis=1, keepdims=True)
        saved = jnp.where(is_grad, 0.0, pick).astype(BF16)
        grads = jnp.where(is_grad, pick, 0.0).astype(BF16)

        def rows_of(at):
            got = jnp.dot(saved, tok[0, :, at], preferred_element_type=F32)
            scaled = jnp.dot(grads, tok[1, :, at], preferred_element_type=F32) * slot_scale
            return (got + scaled).astype(BF16)

        return rows_of

    theirs_of, mine_of = choice(1 - odd_out), choice(odd_out)
    local[0].wait()
    local[1].wait()

    @pl.loop(0, DW // TILE)
    def _(n):
        at = pl.ds(pl.multiple_of(n * TILE, TILE), TILE)
        give[0, :, at] = theirs_of(at)
        give[1, :, at] = mine_of(at)

    local[2].wait()
    local[3].wait()

    def block(owner_x, owner_yh, half=None):
        at = (owner_x * 2 + owner_yh) * SH + (0 if half is None else half * (SH // 2))
        size = SH if half is None else SH // 2
        return pl.ds(pl.multiple_of(at, SH // 2), size)

    mine, theirs = block(x, yh), block(x, 1 - yh)
    lane = lax.broadcasted_iota(jnp.int32, (COLS, 128), 1)
    column = lax.broadcasted_iota(jnp.int32, (COLS, 128), 0) - (lane >> 4) * 64 - (lane & 15)
    for k in range(NK):
        order = jnp.where(column == k * 16, 1.0, 0.0).astype(BF16)
        for a in range(2):
            wts[k, mine, a * 128 : (a + 1) * 128] = jnp.dot(
                raw[a], order, preferred_element_type=F32
            ).astype(BF16)

    place = lax.broadcasted_iota(jnp.int32, (192, 96), 0)
    source = lax.broadcasted_iota(jnp.int32, (192, 96), 1)
    place24 = jnp.zeros((192, 96), jnp.int32)
    for i in range(1, 8):
        place24 = place24 + jnp.where(place >= 24 * i, 1, 0)
    within = place - 24 * place24
    grad12 = jnp.where(within >= 12, 1, 0)
    within = within - 12 * grad12
    second = jnp.where(within >= CAP, 1, 0)
    wanted = place24 * 12 + grad12 * CAP + within - CAP * second
    own_place = jnp.where((wanted == source) & (second == 0), 1.0, 0.0).astype(BF16)
    other_place = jnp.where((wanted == source) & (second == 1), 1.0, 0.0).astype(BF16)

    quarter = c * 16 + par * 8

    pl.semaphore_wait(barrier, 12 + odd_out)
    copy(give.at[0], take, 13, t_recv.at[0], c_dev).start()

    def event_r():
        copy(give.at[0], take, 13, t_recv.at[0], c_dev).wait_recv()

        @pl.loop(0, DW // TILE)
        def _(n):
            at = pl.ds(pl.multiple_of(n * TILE, TILE), TILE)
            both = jnp.dot(own_place, give[1, :, at], preferred_element_type=F32) + jnp.dot(
                other_place, take[:, at], preferred_element_type=F32
            )
            send_rows[:, :, :, at] = both.astype(BF16).reshape(8, 3, 8, TILE)

        for dyl in range(4):
            for j in range(2):
                to_yl, to_zp = lax.rem(yl + dyl, 4), lax.rem(zp + odd_out + 2 * j, 4)
                if j == 0:
                    zi, to_par = odd_out * (1 + par), (1 - odd_out) * par
                else:
                    zi = 3 + odd_out * (par - 2)
                    to_par = (1 - odd_out) * (1 - par) + odd_out
                src = send_rows.at[j * 4 + dyl]
                number = (dyl // 2) * 4 + zi
                dst = rows.at[c * 16 + to_par * 8 + number]
                to = dev(x, yh, to_yl, 2 * to_zp + to_par, c)
                remote = copy(src, dst, 0, d_recv.at[number], to)
                if dyl or j:
                    remote.start()
                else:
                    pl.when(odd_out == 1)(remote.start)

                    @pl.when(odd_out == 0)
                    def _():
                        pltpu.make_async_copy(src, dst, d_recv.at[0]).start()

    def pass_on(k, of_yh, recv, recv_next, sends):
        for s in range(2):
            of_x = ring(x, (-1, 1)[s])
            whole, half = block(of_x, of_yh), block(of_x, of_yh, s)
            copy(wts.at[k, whole], wts.at[k, whole], 3, recv.at[s, k], sides[s]).wait_recv()
            copy(wts.at[k, half], wts.at[k, half], sends, recv_next.at[s, k], sides[s]).start()

    def event_o(k):
        pass_on(k, yh, o_recv, fo_recv, 5)

    def event_p(k):
        pass_on(k, 1 - yh, p_recv, fp_recv, 5)

    def event_u(k):
        for s in range(2):
            copy(wts.at[k, mine], wts.at[k, mine], 3, o_recv.at[s, k], sides[s]).start()

    def event_s(k):
        copy(wts.at[k, mine], wts.at[k, mine], 2, y_recv.at[k], y_dev).start()

    def event_y(k):
        copy(wts.at[k, theirs], wts.at[k, theirs], 2, y_recv.at[k], y_dev).wait_recv()
        for s in range(2):
            copy(wts.at[k, theirs], wts.at[k, theirs], 4, p_recv.at[s, k], sides[s]).start()

    def flatten(first, count):
        at = pl.ds(pl.multiple_of(first * 16, 16), count * 16)
        for a in range(2):
            flat[a, at, :] = rows[pl.ds(first, count), a : a + 2].reshape(count * 16, DW)

    def event_d(number):
        at = quarter + number
        copy(rows.at[at], rows.at[at], 0, d_recv.at[number], z_dev).wait_recv()
        copy(rows.at[at], rows.at[at], 6, z_recv.at[number], z_dev).start()
        copy(rows.at[at], rows.at[at], 8, c_recv.at[0], c_dev).start()
        flatten(at, 1)

    def event_z(number):
        at = c * 16 + (1 - par) * 8 + number
        copy(rows.at[at], rows.at[at], 6, z_recv.at[number], z_dev).wait_recv()
        copy(rows.at[at], rows.at[at], 8, c_recv.at[0], c_dev).start()
        flatten(at, 1)

    def event_x():
        at = pl.ds((1 - c) * 16, 16)
        copy(rows.at[at], rows.at[at], 8, c_recv.at[0], c_dev).wait_recv()

        @pl.loop(0, 8)
        def _(n):
            flatten((1 - c) * 16 + n * 2, 2)

    def owned(of_x, of_yh=None):
        at = of_x * 32 + (0 if of_yh is None else of_yh * 16)
        return pl.ds(pl.multiple_of(at, 16), 32 if of_yh is None else 16)

    def event_c(k):
        for s in range(2):
            for of_yh, recv in ((yh, fo_recv), (1 - yh, fp_recv)):
                half = block(ring(x, 2), of_yh, s)
                copy(wts.at[k, half], wts.at[k, half], 5, recv.at[s, k], sides[s]).wait_recv()
        acc[...] = jnp.zeros_like(acc)

        @pl.loop(0, DW // TILE)
        def _(n):
            at = pl.ds(pl.multiple_of(n * TILE, TILE), TILE)
            acc[...] += jnp.dot(flat[0, :, at], wts[k, at, :], preferred_element_type=F32)

        gate, up = acc[:, 0:128], acc[:, 128:256]
        hidden = jnp.transpose(gate / (1.0 + jnp.exp(-gate)) * up)
        hidden = pltpu.roll(hidden, 4, 1)
        lane16 = lax.broadcasted_iota(jnp.int32, hidden.shape, 1) & 15
        hid_t[...] = jnp.where(lane16 >= 4, hidden, 0.0).astype(BF16)

        @pl.loop(0, DW // TILE)
        def _(n):
            at = pl.ds(pl.multiple_of(n * TILE, TILE), TILE)
            part[k, :, at] = jnp.dot(
                hid_t[...], flat[1, :, at], preferred_element_type=F32
            ).astype(BF16)

        for s in range(2):
            copy(
                part.at[k, owned(ring(x, 2), s)], hop1.at[s, k], 10, h1_recv.at[s, k], sides[s]
            ).start()

    def event_a(k):
        for s in range(2):
            copy(hop1.at[s, k], hop1.at[s, k], 10, h1_recv.at[s, k], sides[s]).wait_recv()
            of_x = ring(x, (1, -1)[s])
            at = owned(of_x, s)
            part[k, at, :] = (
                part[k, at, :].astype(F32) + hop1[s, k].astype(F32)
            ).astype(BF16)
            copy(
                part.at[k, owned(of_x)], hop2.at[s, k], 11, h2_recv.at[s, k], sides[s]
            ).start()

    def event_b(k):
        for s in range(2):
            copy(hop2.at[s, k], hop2.at[s, k], 11, h2_recv.at[s, k], sides[s]).wait_recv()

        def total(of_yh):
            at = pl.ds(pl.multiple_of(of_yh * 16, 16), 16)
            return (
                part[k, owned(x, of_yh), :].astype(F32)
                + hop2[0, k, at, :].astype(F32)
                + hop2[1, k, at, :].astype(F32)
            )

        y_out[k] = total(1 - yh).astype(BF16)
        copy(y_out.at[k], y_in.at[k], 12, ry_recv.at[k], y_dev).start()
        fin[k] = total(yh)

    def event_e(k):
        copy(y_out.at[k], y_in.at[k], 12, ry_recv.at[k], y_dev).wait_recv()
        out_ref[k * 16 : (k + 1) * 16, :] = (fin[k] + y_in[k].astype(F32)).astype(BF16)

    events = dict(
        O=event_o, P=event_p, Y=event_y, S=event_s, U=event_u, D=event_d, Z=event_z, C=event_c,
        A=event_a, B=event_b, E=event_e,
    )
    for name in SCHEDULE:
        if name == "X":
            event_x()
        elif name == "R":
            event_r()
        else:
            events[name[0]](int(name[1]))

    def sent(ref, sends, to):
        copy(ref, ref, sends, o_recv.at[0, 0], to).wait_send()

    sent(give.at[0], 13, c_dev)
    sent(rows.at[pl.ds(0, 8)], 6, z_dev)
    sent(rows.at[pl.ds(0, 16)], 8, c_dev)
    pl.when(odd_out == 0)(lambda: sent(rows.at[pl.ds(0, 7)], 0, z_dev))
    pl.when(odd_out == 1)(lambda: sent(rows.at[pl.ds(0, 8)], 0, z_dev))
    sent(wts.at[0, pl.ds(0, 4 * SH)], 2, y_dev)
    for sends in (3, 4, 5):
        sent(wts.at[0], sends, sides[0])
    sent(flat.at[0, pl.ds(0, 128)], 10, sides[0])
    sent(flat.at[0, pl.ds(0, 256)], 11, sides[0])
    sent(flat.at[0, pl.ds(0, 64)], 12, y_dev)


def per_device(tokens, out_grad, gate_weight, up_weight, route_ids, route_weights):
    vmem = pl.BlockSpec(memory_space=pltpu.VMEM)
    anywhere = pl.BlockSpec(memory_space=pl.ANY)
    dma = pltpu.SemaphoreType.DMA
    return pl.pallas_call(
        kernel,
        out_shape=jax.ShapeDtypeStruct((NK * 16, DW), BF16),
        in_specs=[vmem, vmem, anywhere, anywhere, anywhere, anywhere],
        out_specs=vmem,
        scratch_shapes=[
            pltpu.VMEM((2, TOK, DW), BF16),
            pltpu.VMEM((2, SH, COLS), BF16),
            pltpu.VMEM((2, 96, DW), BF16),
            pltpu.VMEM((96, DW), BF16),
            pltpu.VMEM((8, 3, 8, DW), BF16),
            pltpu.VMEM((32, 3, 8, DW), BF16),
            pltpu.VMEM((2, 512, DW), BF16),
            pltpu.VMEM((NK, 8 * SH, 256), BF16),
            pltpu.VMEM((512, 256), F32),
            pltpu.VMEM((128, 512), BF16),
            pltpu.VMEM((NK, 128, DW), BF16),
            pltpu.VMEM((2, NK, 16, DW), BF16),
            pltpu.VMEM((2, NK, 32, DW), BF16),
            pltpu.VMEM((NK, 16, DW), BF16),
            pltpu.VMEM((NK, 16, DW), BF16),
            pltpu.VMEM((NK, 16, DW), F32),
            dma((4,)),
            dma((1,)),
            dma((NK,)),
            dma((2, NK)),
            dma((2, NK)),
            dma((2, NK)),
            dma((2, NK)),
            dma((8,)),
            dma((8,)),
            dma((1,)),
            dma((2, NK)),
            dma((2, NK)),
            dma((NK,)),
            dma((14,)),
        ],
        compiler_params=pltpu.CompilerParams(
            collective_id=0, has_side_effects=True, vmem_limit_bytes=56 << 20
        ),
        name="routed_grad",
    )(route_ids.T, route_weights.T, tokens, out_grad, gate_weight, up_weight)


def solution(mesh):
    return jax.shard_map(
        per_device,
        mesh=mesh,
        in_specs=(
            P(("dp", "expert"), None),
            P(("dp", "expert"), None),
            P("dp", "expert"),
            P("dp", "expert"),
            P(("dp", "expert"), None),
            P(("dp", "expert"), None),
        ),
        out_specs=P(("expert", "dp"), None),
        check_vma=False,
    )
```

```python
import jax
import jax.numpy as jnp
from jax import lax
from jax.experimental import pallas as pl
from jax.experimental.pallas import tpu as pltpu
from jax.sharding import PartitionSpec as P

MESH = pl.DeviceIdType.MESH
F32 = jnp.float32
BF16 = jnp.bfloat16

TOK = 128
DW = 3584
SH = 448
COLS = 512
CAP = 6
NK = 4
TILE = 512
SCHEDULE = (
    "S0", "U0", "U1", "R", "O0", "U2", "D0", "D1", "O1", "U3", "D2", "Y0", "S1", "P0", "D3",
    "Z0", "Z1", "O2", "D4", "D5", "O3", "Z2", "Z3", "D6", "D7", "Y1", "S2", "P1", "Z4",
    "Z5", "Y2", "S3", "P2", "Z6", "Z7", "Y3", "X", "C0", "P3", "C1", "A0", "C2", "A1", "B0",
    "C3", "A2", "B1", "A3", "B2", "B3", "E0", "E1", "E2", "E3",
)


def kernel(
    ids_ref, rw_ref, tok_hbm, og_hbm, gw_hbm, uw_hbm, out_ref,
    tok, raw, give, take, send_rows, rows, flat, wts, acc, hid_t, part, hop1, hop2, y_out, y_in, fin,
    local_sem, t_recv, y_recv, o_recv, p_recv, fo_recv, fp_recv,
    d_recv, z_recv, c_recv, h1_recv, h2_recv, ry_recv, send_sem,
):
    dp = lax.axis_index("dp")
    ex = lax.axis_index("expert")
    x, yh = dp // 2, lax.rem(dp, 2)
    yl, z, c = ex // 16, lax.rem(ex // 2, 8), lax.rem(ex, 2)
    zp, par = z // 2, lax.rem(z, 2)

    def dev(x_, yh_, yl_, z_, c_):
        return (x_ * 2 + yh_, (yl_ * 8 + z_) * 2 + c_)

    def ring(x_, d):
        return lax.rem(x_ + d + 4, 4)

    sides = (dev(ring(x, 1), yh, yl, z, c), dev(ring(x, -1), yh, yl, z, c))
    y_dev = dev(x, 1 - yh, yl, z, c)
    z_dev = dev(x, yh, yl, z + 1 - 2 * par, c)
    c_dev = dev(x, yh, yl, z, 1 - c)

    def copy(src, dst, sends, recv, to):
        return pltpu.make_async_remote_copy(
            src_ref=src, dst_ref=dst, send_sem=send_sem.at[sends], recv_sem=recv,
            device_id=to, device_id_type=MESH,
        )

    local = [
        pltpu.make_async_copy(tok_hbm, tok.at[0], local_sem.at[0]),
        pltpu.make_async_copy(og_hbm, tok.at[1], local_sem.at[1]),
        pltpu.make_async_copy(gw_hbm, raw.at[0], local_sem.at[2]),
        pltpu.make_async_copy(uw_hbm, raw.at[1], local_sem.at[3]),
    ]
    for one in local:
        one.start()

    barrier = pltpu.get_barrier_semaphore()

    def greet(to):
        pl.semaphore_signal(barrier, inc=1, device_id=to, device_id_type=MESH)

    for to in (*sides, y_dev, z_dev, c_dev):
        greet(to)
    pair = lax.rem(zp + 3 + 2 * par, 4)
    from_z = (z, 2 * pair, 2 * pair + 1, 2 * lax.rem(zp + 2, 4) + 1 - par)
    odd_out = lax.rem(c + yl + zp, 2)
    odd_in = odd_out
    for jj in range(2):
        for zi in range(4):
            to = dev(x, yh, lax.rem(yl + 8 - odd_in - 2 * jj, 4), from_z[zi], c)
            if jj or zi:
                greet(to)
            else:
                pl.when(odd_in == 1)(lambda to=to: greet(to))

    row = lax.broadcasted_iota(jnp.int32, (96, TOK), 0)
    row12 = jnp.zeros((96, TOK), jnp.int32)
    for i in range(1, 8):
        row12 = row12 + jnp.where(row >= 12 * i, 1, 0)
    slot = row - 12 * row12
    is_grad = slot >= CAP
    slot = jnp.where(is_grad, slot - CAP, slot)
    earlier = jnp.where(
        lax.broadcasted_iota(jnp.int32, (TOK, TOK), 0)
        < lax.broadcasted_iota(jnp.int32, (TOK, TOK), 1),
        1.0,
        0.0,
    ).astype(BF16)

    def choice(odd):
        to_zp = (zp + odd + 2 * (row12 >> 2)) & 3
        expert = ((yl + (row12 & 3)) & 3) * 4 + to_zp
        named = jnp.zeros((96, TOK), F32)
        scale = jnp.zeros((96, TOK), F32)
        for k in range(8):
            hit = ids_ref[k : k + 1, :] == expert
            named = jnp.where(hit, 1.0, named)
            scale = scale + jnp.where(hit, rw_ref[k : k + 1, :], 0.0)
        rank = jnp.dot(named.astype(BF16), earlier, preferred_element_type=F32)
        pick = jnp.where(rank == slot.astype(F32), named, 0.0)
        slot_scale = jnp.sum(pick * scale, axis=1, keepdims=True)
        saved = jnp.where(is_grad, 0.0, pick).astype(BF16)
        grads = jnp.where(is_grad, pick, 0.0).astype(BF16)

        def rows_of(at):
            got = jnp.dot(saved, tok[0, :, at], preferred_element_type=F32)
            scaled = jnp.dot(grads, tok[1, :, at], preferred_element_type=F32) * slot_scale
            return (got + scaled).astype(BF16)

        return rows_of

    theirs_of, mine_of = choice(1 - odd_out), choice(odd_out)
    local[0].wait()
    local[1].wait()

    @pl.loop(0, DW // TILE)
    def _(n):
        at = pl.ds(pl.multiple_of(n * TILE, TILE), TILE)
        give[0, :, at] = theirs_of(at)
        give[1, :, at] = mine_of(at)

    local[2].wait()
    local[3].wait()

    def block(owner_x, owner_yh, half=None):
        at = (owner_x * 2 + owner_yh) * SH + (0 if half is None else half * (SH // 2))
        size = SH if half is None else SH // 2
        return pl.ds(pl.multiple_of(at, SH // 2), size)

    mine, theirs = block(x, yh), block(x, 1 - yh)
    lane = lax.broadcasted_iota(jnp.int32, (COLS, 128), 1)
    column = lax.broadcasted_iota(jnp.int32, (COLS, 128), 0) - (lane >> 4) * 64 - (lane & 15)
    for k in range(NK):
        order = jnp.where(column == k * 16, 1.0, 0.0).astype(BF16)
        for a in range(2):
            wts[k, mine, a * 128 : (a + 1) * 128] = jnp.dot(
                raw[a], order, preferred_element_type=F32
            ).astype(BF16)

    place = lax.broadcasted_iota(jnp.int32, (192, 96), 0)
    source = lax.broadcasted_iota(jnp.int32, (192, 96), 1)
    place24 = jnp.zeros((192, 96), jnp.int32)
    for i in range(1, 8):
        place24 = place24 + jnp.where(place >= 24 * i, 1, 0)
    within = place - 24 * place24
    grad12 = jnp.where(within >= 12, 1, 0)
    within = within - 12 * grad12
    second = jnp.where(within >= CAP, 1, 0)
    wanted = place24 * 12 + grad12 * CAP + within - CAP * second
    own_place = jnp.where((wanted == source) & (second == 0), 1.0, 0.0).astype(BF16)
    other_place = jnp.where((wanted == source) & (second == 1), 1.0, 0.0).astype(BF16)

    quarter = c * 16 + par * 8

    pl.semaphore_wait(barrier, 12 + odd_out)
    copy(give.at[0], take, 13, t_recv.at[0], c_dev).start()

    def event_r():
        copy(give.at[0], take, 13, t_recv.at[0], c_dev).wait_recv()

        @pl.loop(0, DW // TILE)
        def _(n):
            at = pl.ds(pl.multiple_of(n * TILE, TILE), TILE)
            both = jnp.dot(own_place, give[1, :, at], preferred_element_type=F32) + jnp.dot(
                other_place, take[:, at], preferred_element_type=F32
            )
            send_rows[:, :, :, at] = both.astype(BF16).reshape(8, 3, 8, TILE)

        for j in range(2):
            for dyl in range(4):
                to_yl, to_zp = lax.rem(yl + dyl, 4), lax.rem(zp + odd_out + 2 * j, 4)
                if j == 0:
                    zi, to_par = odd_out * (1 + par), (1 - odd_out) * par
                else:
                    zi = 3 + odd_out * (par - 2)
                    to_par = (1 - odd_out) * (1 - par) + odd_out
                src = send_rows.at[j * 4 + dyl]
                number = (dyl // 2) * 4 + zi
                dst = rows.at[c * 16 + to_par * 8 + number]
                to = dev(x, yh, to_yl, 2 * to_zp + to_par, c)
                remote = copy(src, dst, 0, d_recv.at[number], to)
                if dyl or j:
                    remote.start()
                else:
                    pl.when(odd_out == 1)(remote.start)

                    @pl.when(odd_out == 0)
                    def _():
                        pltpu.make_async_copy(src, dst, d_recv.at[0]).start()

    def pass_on(k, of_yh, recv, recv_next, sends):
        for s in range(2):
            of_x = ring(x, (-1, 1)[s])
            whole, half = block(of_x, of_yh), block(of_x, of_yh, s)
            copy(wts.at[k, whole], wts.at[k, whole], 3, recv.at[s, k], sides[s]).wait_recv()
            copy(wts.at[k, half], wts.at[k, half], sends, recv_next.at[s, k], sides[s]).start()

    def event_o(k):
        pass_on(k, yh, o_recv, fo_recv, 5)

    def event_p(k):
        pass_on(k, 1 - yh, p_recv, fp_recv, 5)

    def event_u(k):
        for s in range(2):
            copy(wts.at[k, mine], wts.at[k, mine], 3, o_recv.at[s, k], sides[s]).start()

    def event_s(k):
        copy(wts.at[k, mine], wts.at[k, mine], 2, y_recv.at[k], y_dev).start()

    def event_y(k):
        copy(wts.at[k, theirs], wts.at[k, theirs], 2, y_recv.at[k], y_dev).wait_recv()
        for s in range(2):
            copy(wts.at[k, theirs], wts.at[k, theirs], 4, p_recv.at[s, k], sides[s]).start()

    def flatten(first, count):
        at = pl.ds(pl.multiple_of(first * 16, 16), count * 16)
        for a in range(2):
            flat[a, at, :] = rows[pl.ds(first, count), a : a + 2].reshape(count * 16, DW)

    def event_d(number):
        at = quarter + number
        copy(rows.at[at], rows.at[at], 0, d_recv.at[number], z_dev).wait_recv()
        copy(rows.at[at], rows.at[at], 6, z_recv.at[number], z_dev).start()
        copy(rows.at[at], rows.at[at], 8, c_recv.at[0], c_dev).start()
        flatten(at, 1)

    def event_z(number):
        at = c * 16 + (1 - par) * 8 + number
        copy(rows.at[at], rows.at[at], 6, z_recv.at[number], z_dev).wait_recv()
        copy(rows.at[at], rows.at[at], 8, c_recv.at[0], c_dev).start()
        flatten(at, 1)

    def event_x():
        at = pl.ds((1 - c) * 16, 16)
        copy(rows.at[at], rows.at[at], 8, c_recv.at[0], c_dev).wait_recv()

        @pl.loop(0, 8)
        def _(n):
            flatten((1 - c) * 16 + n * 2, 2)

    def owned(of_x, of_yh=None):
        at = of_x * 32 + (0 if of_yh is None else of_yh * 16)
        return pl.ds(pl.multiple_of(at, 16), 32 if of_yh is None else 16)

    def event_c(k):
        for s in range(2):
            for of_yh, recv in ((yh, fo_recv), (1 - yh, fp_recv)):
                half = block(ring(x, 2), of_yh, s)
                copy(wts.at[k, half], wts.at[k, half], 5, recv.at[s, k], sides[s]).wait_recv()
        acc[...] = jnp.zeros_like(acc)

        @pl.loop(0, DW // 896)
        def _(n):
            at = pl.ds(pl.multiple_of(n * 896, 896), 896)
            acc[...] += jnp.dot(flat[0, :, at], wts[k, at, :], preferred_element_type=F32)

        gate, up = acc[:, 0:128], acc[:, 128:256]
        hidden = jnp.transpose(gate / (1.0 + jnp.exp(-gate)) * up)
        hidden = pltpu.roll(hidden, 4, 1)
        lane16 = lax.broadcasted_iota(jnp.int32, hidden.shape, 1) & 15
        hid_t[...] = jnp.where(lane16 >= 4, hidden, 0.0).astype(BF16)

        @pl.loop(0, DW // 896)
        def _(n):
            at = pl.ds(pl.multiple_of(n * 896, 896), 896)
            part[k, :, at] = jnp.dot(
                hid_t[...], flat[1, :, at], preferred_element_type=F32
            ).astype(BF16)

        for s in range(2):
            copy(
                part.at[k, owned(ring(x, 2), s)], hop1.at[s, k], 10, h1_recv.at[s, k], sides[s]
            ).start()

    def event_a(k):
        for s in range(2):
            copy(hop1.at[s, k], hop1.at[s, k], 10, h1_recv.at[s, k], sides[s]).wait_recv()
            of_x = ring(x, (1, -1)[s])
            at = owned(of_x, s)
            part[k, at, :] = (
                part[k, at, :].astype(F32) + hop1[s, k].astype(F32)
            ).astype(BF16)
            copy(
                part.at[k, owned(of_x)], hop2.at[s, k], 11, h2_recv.at[s, k], sides[s]
            ).start()

    def event_b(k):
        for s in range(2):
            copy(hop2.at[s, k], hop2.at[s, k], 11, h2_recv.at[s, k], sides[s]).wait_recv()

        def total(of_yh):
            at = pl.ds(pl.multiple_of(of_yh * 16, 16), 16)
            return (
                part[k, owned(x, of_yh), :].astype(F32)
                + hop2[0, k, at, :].astype(F32)
                + hop2[1, k, at, :].astype(F32)
            )

        y_out[k] = total(1 - yh).astype(BF16)
        copy(y_out.at[k], y_in.at[k], 12, ry_recv.at[k], y_dev).start()
        fin[k] = total(yh)

    def event_e(k):
        copy(y_out.at[k], y_in.at[k], 12, ry_recv.at[k], y_dev).wait_recv()
        out_ref[k * 16 : (k + 1) * 16, :] = (fin[k] + y_in[k].astype(F32)).astype(BF16)

    events = dict(
        O=event_o, P=event_p, Y=event_y, S=event_s, U=event_u, D=event_d, Z=event_z, C=event_c,
        A=event_a, B=event_b, E=event_e,
    )
    for name in SCHEDULE:
        if name == "X":
            event_x()
        elif name == "R":
            event_r()
        else:
            events[name[0]](int(name[1]))

    def sent(ref, sends, to):
        copy(ref, ref, sends, o_recv.at[0, 0], to).wait_send()

    sent(give.at[0], 13, c_dev)
    sent(rows.at[pl.ds(0, 8)], 6, z_dev)
    sent(rows.at[pl.ds(0, 16)], 8, c_dev)
    pl.when(odd_out == 0)(lambda: sent(rows.at[pl.ds(0, 7)], 0, z_dev))
    pl.when(odd_out == 1)(lambda: sent(rows.at[pl.ds(0, 8)], 0, z_dev))
    sent(wts.at[0, pl.ds(0, 4 * SH)], 2, y_dev)
    for sends in (3, 4, 5):
        sent(wts.at[0], sends, sides[0])
    sent(flat.at[0, pl.ds(0, 128)], 10, sides[0])
    sent(flat.at[0, pl.ds(0, 256)], 11, sides[0])
    sent(flat.at[0, pl.ds(0, 64)], 12, y_dev)


def per_device(tokens, out_grad, gate_weight, up_weight, route_ids, route_weights):
    vmem = pl.BlockSpec(memory_space=pltpu.VMEM)
    anywhere = pl.BlockSpec(memory_space=pl.ANY)
    dma = pltpu.SemaphoreType.DMA
    return pl.pallas_call(
        kernel,
        out_shape=jax.ShapeDtypeStruct((NK * 16, DW), BF16),
        in_specs=[vmem, vmem, anywhere, anywhere, anywhere, anywhere],
        out_specs=vmem,
        scratch_shapes=[
            pltpu.VMEM((2, TOK, DW), BF16),
            pltpu.VMEM((2, SH, COLS), BF16),
            pltpu.VMEM((2, 96, DW), BF16),
            pltpu.VMEM((96, DW), BF16),
            pltpu.VMEM((8, 3, 8, DW), BF16),
            pltpu.VMEM((32, 3, 8, DW), BF16),
            pltpu.VMEM((2, 512, DW), BF16),
            pltpu.VMEM((NK, 8 * SH, 256), BF16),
            pltpu.VMEM((512, 256), F32),
            pltpu.VMEM((128, 512), BF16),
            pltpu.VMEM((NK, 128, DW), BF16),
            pltpu.VMEM((2, NK, 16, DW), BF16),
            pltpu.VMEM((2, NK, 32, DW), BF16),
            pltpu.VMEM((NK, 16, DW), BF16),
            pltpu.VMEM((NK, 16, DW), BF16),
            pltpu.VMEM((NK, 16, DW), F32),
            dma((4,)),
            dma((1,)),
            dma((NK,)),
            dma((2, NK)),
            dma((2, NK)),
            dma((2, NK)),
            dma((2, NK)),
            dma((8,)),
            dma((8,)),
            dma((1,)),
            dma((2, NK)),
            dma((2, NK)),
            dma((NK,)),
            dma((14,)),
        ],
        compiler_params=pltpu.CompilerParams(
            collective_id=0, has_side_effects=True, vmem_limit_bytes=56 << 20
        ),
        name="routed_grad",
    )(route_ids.T, route_weights.T, tokens, out_grad, gate_weight, up_weight)


def solution(mesh):
    return jax.shard_map(
        per_device,
        mesh=mesh,
        in_specs=(
            P(("dp", "expert"), None),
            P(("dp", "expert"), None),
            P("dp", "expert"),
            P("dp", "expert"),
            P(("dp", "expert"), None),
            P(("dp", "expert"), None),
        ),
        out_specs=P(("expert", "dp"), None),
        check_vma=False,
    )
```
